32 devices in a mesh: clip: 2 (over x), tile: 16 (over z, y, core).
Axes of the slice: x: 2, y: 2, z: 4, core: 2. Of those that a mesh axis runs over, the one named last changes fastest.
Arguments:
- latent: bfloat16 [8, 128, 32, 128], P('clip', 'tile'), parts along dimension 0, may hold values from -6 to 6
- cotangent: bfloat16 [8, 256, 64, 128], P('clip', 'tile'), parts along dimension 0, may hold values from -6 to 6
- kernel: bfloat16 [3, 3, 3, 128, 128], replicated, may hold values from -0.109375 to 0.109375
- ramp_lengths: int32 [32], P('clip'), parts along dimension 0, may hold values from 1 to 4
Outputs:
- latent_grad: bfloat16 [8, 128, 32, 128], P('clip', 'tile'), parts along dimension 0
- kernel_grad: float32 [256, 3456], P(('clip', 'tile')), parts along dimension 0
The draws below stay inside these ranges and needn't reach their ends.
There are 2 independent parts, one for each index of `clip`. The reference program is written for one: setup_inputs(seed, part) draws one part's arguments, and reference() takes and returns one part's arrays. A program takes and returns all parts, laid end to end along the dimension named above; an argument that names none is the same for every part. Nothing has to cross between parts.
Inputs may be any that keep to these rules, and one draw needn't show every extreme that they name: `ramp_lengths`: entry t (t >= 1) is the ramp length of the boundary between tiles t - 1 and t; entry 0 is not used.
All inputs are finite; a program needn't handle non-finite values.
Results may differ from the reference program's by a relative error of at most 0.0031.
Values may be sent and summed in bfloat16 or wider, within the bound.
A program may use at most 128 MiB of HBM per device.

```python
import math
import jax
import jax.numpy as jnp
from jax import lax

C = 128
F = 4
R = 8
COLS = 32
OV = 1
NR = 128
N_TILE = 16


def place_ends(values, key, smallest, top_value):
    index_at = [jax.random.randint(jax.random.fold_in(key, axis), (), 0, length) for axis, length in enumerate(values.shape)]
    main_axis = values.shape.index(max(values.shape))
    beside = index_at[:main_axis] + [(index_at[main_axis] + 1) % values.shape[main_axis]] + index_at[main_axis + 1:]
    return values.at[tuple(index_at)].set(smallest).at[tuple(beside)].set(top_value)


def levels(key, extent, cuts, least, high):
    factor_of, own = 1.0, jax.random.fold_in(key, 6)
    for position, parts in cuts:
        heights = jnp.exp(jax.random.uniform(jax.random.fold_in(own, position), (parts,), jnp.float32, least / len(cuts), high / len(cuts)))
        factor_of = factor_of * jnp.repeat(heights, extent[position] // parts).reshape([-1 if axis == position else 1 for axis in range(len(extent))])
    return factor_of


def normal_values(own_key, shape, deviation, most, pieces=(), kind=jnp.bfloat16):
    values = deviation * jax.random.normal(own_key, shape, jnp.float32)
    if pieces:
        values = values * levels(own_key, shape, pieces, -0.22, 0.18)
    return jnp.clip(values, -most, most).astype(kind)


def setup_inputs(seed: int = 0, part: int = 0) -> dict:
    splits = jax.random.split(jax.random.key(seed), 5)
    own_keys = jax.random.split(jax.random.fold_in(splits[4], part), 5)
    return {
        "latent": normal_values(own_keys[0], (F, NR, COLS, C), 1.0, 6.0, ((1, 16),)),
        "cotangent": normal_values(own_keys[1], (F, 2 * NR, 2 * COLS, C), 1.0, 6.0, ((1, 16),)),
        "kernel": normal_values(splits[2], (3, 3, 3, C, C), (27 * C) ** -0.5, 0.109375),
        "ramp_lengths": place_ends(jax.random.randint(own_keys[3], (N_TILE,), 1, 4 * OV + 1), jax.random.fold_in(own_keys[3], 1), 1, 4 * OV).astype(jnp.int32),
    }


def rise(offset, length):
    shift_rows = (4 * OV - length) // 2
    value = (offset - shift_rows + 1).astype(jnp.float32) / (length + 1).astype(jnp.float32)
    return jnp.clip(value, 0.0, 1.0)

def blend_rows(rows_local, band_out, tile_id, tiles, ramp_lengths):
    lower_len = ramp_lengths[tile_id]
    upper_len = ramp_lengths[jnp.minimum(tile_id + 1, tiles - 1)]
    low_factor = jnp.where(tile_id >= 1, rise(rows_local, lower_len), jnp.float32(1.0))
    high_factor = jnp.where(tile_id <= tiles - 2, 1.0 - rise(rows_local - band_out, upper_len), jnp.float32(1.0))
    return (low_factor * high_factor).astype(jnp.float32)

def upsample(values):
    return jnp.repeat(jnp.repeat(values, 2, axis=1), 2, axis=2)

def spread_back(grad_rows, kernel):
    frames, rows_n, width, chans = grad_rows.shape
    padded = jnp.pad(grad_rows, ((0, 2), (2, 2), (1, 1), (0, 0)))
    summed = jnp.zeros((frames * (rows_n + 2) * width, chans), jnp.float32)
    for frame_tap in range(3):
        for row_tap in range(3):
            for col_tap in range(3):
                window = padded[2 - frame_tap:2 - frame_tap + frames, 2 - row_tap:2 - row_tap + rows_n + 2, 2 - col_tap:2 - col_tap + width]
                summed = summed + lax.dot_general(window.reshape(-1, chans), kernel[frame_tap, row_tap, col_tap], (((1,), (1,)), ((), ())), preferred_element_type=jnp.float32)
    return summed.reshape(frames, rows_n + 2, width, chans)

def kernel_terms(grad_rows, up_rows, chan_first, chan_count):
    frames, rows_n, width, chans = grad_rows.shape
    padded = jnp.pad(up_rows, ((2, 0), (0, 0), (1, 1), (0, 0)))
    padded = lax.dynamic_slice_in_dim(padded, chan_first, chan_count, 3)
    flat_grad = grad_rows.reshape(-1, chans)
    blocks = []
    for frame_tap in range(3):
        for row_tap in range(3):
            for col_tap in range(3):
                window = padded[frame_tap:frame_tap + frames, row_tap:row_tap + rows_n, col_tap:col_tap + width]
                blocks.append(lax.dot_general(window.reshape(-1, chan_count), flat_grad, (((0,), (0,)), ((), ())), preferred_element_type=jnp.float32))
    return jnp.concatenate(blocks, axis=1)

def pool_pairs(values):
    frames, rows_n, width, chans = values.shape
    return values.reshape(frames, rows_n // 2, 2, width // 2, 2, chans).sum(axis=(2, 4))

def reference(latent, cotangent, kernel, ramp_lengths):
    frames, rows_all, width, chans = latent.shape
    tiles = N_TILE
    ext_rows = 2 * R + 4 * OV
    lat_pad = jnp.pad(latent, ((0, 0), (OV, OV), (0, 0), (0, 0)))
    cot_pad = jnp.pad(cotangent, ((0, 0), (2 * OV, 2 * OV), (0, 0), (0, 0)))
    rows_local = jnp.arange(ext_rows, dtype=jnp.int32)

    def one_tile(carry, tile_id):
        grad_sum, kernel_sum = carry
        lat_ext = lax.dynamic_slice_in_dim(lat_pad, (tile_id * R).astype(jnp.int32), R + 2 * OV, 1)
        cot_ext = lax.dynamic_slice_in_dim(cot_pad, (tile_id * 2 * R).astype(jnp.int32), ext_rows, 1)
        weights = blend_rows(rows_local, 2 * R, tile_id, tiles, ramp_lengths)
        grad_w = (cot_ext.astype(jnp.float32) * weights[None, :, None, None]).astype(jnp.bfloat16)
        up_pad = jnp.pad(upsample(lat_ext), ((0, 0), (1, 1), (0, 0), (0, 0)))
        grad_up = spread_back(grad_w, kernel)[:, 1:ext_rows + 1]
        pooled = pool_pairs(grad_up)
        offset = (tile_id * R).astype(jnp.int32)
        current = lax.dynamic_slice_in_dim(grad_sum, offset, R + 2 * OV, 1)
        grad_sum = lax.dynamic_update_slice_in_dim(grad_sum, current + pooled, offset, 1)
        kernel_sum = kernel_sum + kernel_terms(grad_w, up_pad, 0, chans)
        return ((grad_sum, kernel_sum), None)
    init = (jnp.zeros((frames, rows_all + 2 * OV, width, chans), jnp.float32), jnp.zeros((chans, 27 * chans), jnp.float32))
    (grad_sum, kernel_sum), unused = lax.scan(one_tile, init, jnp.arange(tiles, dtype=jnp.int32))
    latent_grad = grad_sum[:, OV:OV + rows_all].astype(jnp.bfloat16)
    kernel_grad = kernel_sum / jnp.float32(math.sqrt(4 * frames * rows_all * width))
    return (latent_grad, kernel_grad)
```

```python
import functools
import math

import jax
import jax.numpy as jnp
from jax import lax
from jax.experimental import pallas as pl
from jax.experimental.pallas import tpu as pltpu
from jax.sharding import PartitionSpec as P

OV = 1
MESH = pl.DeviceIdType.MESH
F32 = jnp.float32
BF16 = jnp.bfloat16
EDGE = 8


def rise(offset, length):
    shift_rows = lax.shift_right_arithmetic(4 * OV - length, jnp.ones_like(length))
    value = (offset - shift_rows + 1).astype(F32) / (length + 1).astype(F32)
    return jnp.clip(value, 0.0, 1.0)


def body(tiles, fused, norm, ramp_ref, lat_ref, cot_ref, k_ref, lg_ref, kg_ref, *scratch):
    if fused:
        (halo_lo, halo_hi, pad, lhs, gh, gl, kt_ref, halo_send, halo_recv,
         part, core_buf, send_buf, recv_buf, core_send, core_recv, far_send, far_recv) = scratch
    else:
        halo_lo, halo_hi, pad, lhs, gh, gl, kt_ref, halo_send, halo_recv = scratch
    frames, band, width, chans = lat_ref.shape
    wide = 2 * width
    area = band * width
    me = lax.axis_index("tile")
    core = lax.rem(me, 2)
    chip = lax.div(me, 2)
    chips = tiles // 2
    share = chans // tiles

    halo_lo[...] = jnp.zeros_like(halo_lo)
    halo_hi[...] = jnp.zeros_like(halo_hi)
    barrier = pltpu.get_barrier_semaphore()
    for d in range(1, tiles):
        pl.semaphore_signal(
            barrier, inc=1, device_id={"tile": lax.rem(me + d, tiles)}, device_id_type=MESH
        )

    for f in range(frames):
        turned = lat_ref[f].reshape(area, chans).T
        for kt in range(3):
            g_frame = f + 2 - kt
            if g_frame < frames:
                lhs[kt * chans : (kt + 1) * chans, g_frame * area : (g_frame + 1) * area] = turned
    for kt in range(2):
        for g_frame in range(2 - kt):
            lhs[kt * chans : (kt + 1) * chans, g_frame * area : (g_frame + 1) * area] = jnp.zeros(
                (chans, area), BF16
            )
    pad[:, :EDGE] = jnp.zeros((band, EDGE, chans), F32)
    pad[:, EDGE + wide :] = jnp.zeros((band, EDGE, chans), F32)
    upper = jnp.full((1, chans), ramp_ref[lax.min(me + 1, tiles - 1)], jnp.int32)
    lower = jnp.full((1, chans), ramp_ref[me], jnp.int32)
    has_upper = jnp.where(me <= tiles - 2, 1.0, 0.0).astype(F32)
    has_lower = jnp.where(me >= 1, 1.0, 0.0).astype(F32)
    upper_w = 1.0 - has_upper * rise(jnp.zeros_like(upper), upper)
    lower_w = 1.0 - has_lower * (1.0 - rise(jnp.full_like(lower, 3), lower))

    pl.semaphore_wait(barrier, tiles - 1)

    to_upper = pltpu.make_async_remote_copy(
        src_ref=cot_ref.at[:, 2 * band - 1], dst_ref=halo_lo, send_sem=halo_send.at[0],
        recv_sem=halo_recv.at[0], device_id={"tile": lax.rem(me + 1, tiles)}, device_id_type=MESH,
    )
    to_lower = pltpu.make_async_remote_copy(
        src_ref=cot_ref.at[:, 0], dst_ref=halo_hi, send_sem=halo_send.at[1],
        recv_sem=halo_recv.at[1], device_id={"tile": lax.rem(me + tiles - 1, tiles)}, device_id_type=MESH,
    )

    @pl.when(me < tiles - 1)
    def _():
        to_upper.start()

    @pl.when(me > 0)
    def _():
        to_lower.start()

    def build(kr):
        def one_frame(f, carry):
            for q in range(band):
                first, second = 2 * q + 1 - kr, 2 * q + 2 - kr
                low = (halo_lo[f] if first < 0 else cot_ref[f, first]).astype(F32)
                high = (halo_hi[f] if second == 2 * band else cot_ref[f, second]).astype(F32)
                if kr == 0 and q == band - 2:
                    high = high * upper_w
                if kr == 2 and q == 1:
                    low = low * lower_w
                pad[q, EDGE : EDGE + wide] = low + high
                left = pad[q, pl.ds(EDGE - 1, width, stride=2)]
                even = pad[q, pl.ds(EDGE, width, stride=2)]
                odd = pad[q, pl.ds(EDGE + 1, width, stride=2)]
                right = pad[q, pl.ds(EDGE + 2, width, stride=2)]
                rows = pl.ds(pl.multiple_of(f * area + q * width, width), width)
                for kc, box in enumerate((odd + right, even + odd, left + even)):
                    top = box.astype(BF16)
                    gh[kr, rows, kc * chans : (kc + 1) * chans] = top
                    gl[kr, rows, kc * chans : (kc + 1) * chans] = (box - top.astype(F32)).astype(BF16)
            return carry

        lax.fori_loop(0, frames, one_frame, 0)

    def core_copy(kr):
        return pltpu.make_async_remote_copy(
            src_ref=part.at[kr, 1 - core], dst_ref=core_buf.at[kr], send_sem=core_send.at[kr],
            recv_sem=core_recv.at[kr], device_id={"tile": me + 1 - 2 * core}, device_id_type=MESH,
        )

    def far_copy(kr, d):
        target = lax.rem(chip + d, chips)
        return pltpu.make_async_remote_copy(
            src_ref=send_buf.at[kr, target], dst_ref=recv_buf.at[kr, d - 1],
            send_sem=far_send.at[kr, d - 1], recv_sem=far_recv.at[kr, d - 1],
            device_id={"tile": 2 * target + core}, device_id_type=MESH,
        )

    def kernel_part(kr):
        total = jnp.dot(lhs[...], gh[kr], preferred_element_type=F32)
        total = total + jnp.dot(lhs[...], gl[kr], preferred_element_type=F32)
        for kt in range(3):
            if fused:
                for owner in range(tiles):
                    start = kt * chans + owner * share
                    part[kr, owner % 2, owner // 2, kt] = total[start : start + share]
            else:
                kg_ref[:, (kt * 3 + kr) * 3 * chans : (kt * 3 + kr + 1) * 3 * chans] = total[
                    kt * chans : (kt + 1) * chans
                ]
        if fused:
            core_copy(kr).start()

    def pass_on(kr):
        if fused:
            core_copy(kr).wait_recv()
            send_buf[kr] = (part[kr, core] + core_buf[kr]).astype(BF16)
            for d in range(1, chips):
                far_copy(kr, d).start()

    build(1)
    kernel_part(1)

    @pl.when(me > 0)
    def _():
        to_upper.wait_recv()

    @pl.when(me < tiles - 1)
    def _():
        to_lower.wait_recv()

    build(0)
    pass_on(1)
    kernel_part(0)
    build(2)
    pass_on(0)
    kernel_part(2)

    for kr in range(3):
        for kc in range(3):
            for kt in range(3):
                kt_ref[kr, kc * chans : (kc + 1) * chans, kt * chans : (kt + 1) * chans] = k_ref[kt, kr, kc].T
    pass_on(2)

    sums = [None] * frames
    for f in range(frames):
        first_kt = max(0, 2 - f)
        rows = slice(f * area, (f + 1) * area)
        spread = jnp.zeros((area, (3 - first_kt) * chans), F32)
        for kr in range(3):
            taps = kt_ref[kr, :, first_kt * chans :]
            spread = spread + jnp.dot(gh[kr, rows], taps, preferred_element_type=F32)
            spread = spread + jnp.dot(gl[kr, rows], taps, preferred_element_type=F32)
        for kt in range(first_kt, 3):
            term = spread[:, (kt - first_kt) * chans : (kt - first_kt + 1) * chans]
            target = f - 2 + kt
            sums[target] = term if sums[target] is None else sums[target] + term
    for f in range(frames):
        lg_ref[f] = sums[f].astype(BF16).reshape(band, width, chans)

    @pl.when(me < tiles - 1)
    def _():
        to_upper.wait_send()

    @pl.when(me > 0)
    def _():
        to_lower.wait_send()

    if fused:
        for kr in (1, 0, 2):
            for d in range(1, chips):
                far_copy(kr, d).wait_recv()
            for kt in range(3):
                total = part[kr, core, chip, kt] + core_buf[kr, chip, kt]
                for d in range(1, chips):
                    total = total + recv_buf[kr, d - 1, kt].astype(F32)
                start = (kt * 3 + kr) * 3 * chans
                kg_ref[:, start : start + 3 * chans] = total / F32(norm)
        for kr in range(3):
            core_copy(kr).wait_send()
            for d in range(1, chips):
                far_copy(kr, d).wait_send()


def shards(tiles, latent, cotangent, kernel, ramp_lengths):
    frames, band, width, chans = latent.shape
    share = chans // tiles
    norm = math.sqrt(4 * frames * band * tiles * width)
    fused = share % 8 == 0 and tiles % 2 == 0
    chips = tiles // 2
    cols = 27 * chans
    dma = pltpu.SemaphoreType.DMA
    scratch = [
        pltpu.VMEM((frames, 2 * width, chans), BF16),
        pltpu.VMEM((frames, 2 * width, chans), BF16),
        pltpu.VMEM((band, 2 * width + 2 * EDGE, chans), F32),
        pltpu.VMEM((3 * chans, frames * band * width), BF16),
        pltpu.VMEM((3, frames * band * width, 3 * chans), BF16),
        pltpu.VMEM((3, frames * band * width, 3 * chans), BF16),
        pltpu.VMEM((3, 3 * chans, 3 * chans), BF16),
        dma((2,)),
        dma((2,)),
    ]
    if fused:
        scratch += [
            pltpu.VMEM((3, 2, chips, 3, share, 3 * chans), F32),
            pltpu.VMEM((3, chips, 3, share, 3 * chans), F32),
            pltpu.VMEM((3, chips, 3, share, 3 * chans), BF16),
            pltpu.VMEM((3, chips - 1, 3, share, 3 * chans), BF16),
            dma((3,)),
            dma((3,)),
            dma((3, chips - 1)),
            dma((3, chips - 1)),
        ]
    vmem = pl.BlockSpec(memory_space=pltpu.VMEM)
    latent_grad, kernel_grad = pl.pallas_call(
        functools.partial(body, tiles, fused, norm),
        out_shape=(
            jax.ShapeDtypeStruct(latent.shape, BF16),
            jax.ShapeDtypeStruct((share if fused else chans, cols), F32),
        ),
        in_specs=[pl.BlockSpec(memory_space=pltpu.SMEM), vmem, vmem, vmem],
        out_specs=(vmem, vmem),
        scratch_shapes=scratch,
        compiler_params=pltpu.CompilerParams(
            collective_id=0, has_side_effects=True, vmem_limit_bytes=48 * 2**20
        ),
    )(ramp_lengths, latent, cotangent, kernel)
    if not fused:
        kernel_grad = lax.psum_scatter(kernel_grad, "tile", scatter_dimension=0, tiled=True) / F32(norm)
    return latent_grad, kernel_grad


def solution(mesh):
    in_specs = (P("clip", "tile", None, None), P("clip", "tile", None, None), P(), P("clip"))
    out_specs = (P("clip", "tile", None, None), P(("clip", "tile"), None))
    return jax.shard_map(
        functools.partial(shards, mesh.shape["tile"]),
        mesh=mesh, in_specs=in_specs, out_specs=out_specs, check_vma=False,
    )
```

```python
import functools
import math

import jax
import jax.numpy as jnp
from jax import lax
from jax.experimental import pallas as pl
from jax.experimental.pallas import tpu as pltpu
from jax.sharding import PartitionSpec as P

OV = 1
MESH = pl.DeviceIdType.MESH
F32 = jnp.float32
BF16 = jnp.bfloat16
EDGE = 8


def rise(offset, length):
    shift_rows = lax.shift_right_arithmetic(4 * OV - length, jnp.ones_like(length))
    value = (offset - shift_rows + 1).astype(F32) / (length + 1).astype(F32)
    return jnp.clip(value, 0.0, 1.0)


def body(tiles, fused, norm, ramp_in, lat_in, cot_in, k_in, lg_ref, kg_ref, *scratch):
    (ramp_ref, lat_ref, cot_ref, k_ref, in_sem, cot_sem, halo_lo, halo_hi, pad, lhs, gh, gl, kt_ref,
     halo_send, halo_recv) = scratch[:15]
    if fused:
        (part, core_buf, send_buf, recv_buf, core_send, core_recv, far_send, far_recv) = scratch[15:]
    frames, band, width, chans = lat_ref.shape
    wide = 2 * width
    area = band * width
    me = lax.axis_index("tile")
    core = lax.rem(me, 2)
    chip = lax.div(me, 2)
    chips = tiles // 2
    share = chans // tiles

    def cot_frame(f):
        return pltpu.make_async_copy(cot_in.at[f], cot_ref.at[f], cot_sem.at[f])

    ramp_copy = pltpu.make_async_copy(ramp_in, ramp_ref, in_sem.at[0])
    lat_copy = pltpu.make_async_copy(lat_in, lat_ref, in_sem.at[1])
    k_copy = pltpu.make_async_copy(k_in, k_ref, in_sem.at[2])
    ramp_copy.start()
    for f in range(frames):
        cot_frame(f).start()
    lat_copy.start()
    k_copy.start()

    halo_lo[...] = jnp.zeros_like(halo_lo)
    halo_hi[...] = jnp.zeros_like(halo_hi)
    barrier = pltpu.get_barrier_semaphore()
    for d in range(1, tiles):
        pl.semaphore_signal(
            barrier, inc=1, device_id={"tile": lax.rem(me + d, tiles)}, device_id_type=MESH
        )

    pad[:, :EDGE] = jnp.zeros((band + 3, EDGE, chans), F32)
    pad[:, EDGE + wide :] = jnp.zeros((band + 3, EDGE, chans), F32)
    def box_row(f, slot, low, high, targets):
        pad[slot, EDGE : EDGE + wide] = low + high
        left = pad[slot, pl.ds(EDGE - 1, width, stride=2)]
        even = pad[slot, pl.ds(EDGE, width, stride=2)]
        odd = pad[slot, pl.ds(EDGE + 1, width, stride=2)]
        right = pad[slot, pl.ds(EDGE + 2, width, stride=2)]
        for kc, box in enumerate((odd + right, even + odd, left + even)):
            cols = slice(kc * chans, (kc + 1) * chans)
            top = box.astype(BF16)
            rest = (box - top.astype(F32)).astype(BF16)
            for kr, q in targets:
                rows = pl.ds(pl.multiple_of(f * area + q * width, width), width)
                gh[kr, rows, cols] = top
                gl[kr, rows, cols] = rest

    def build_middle(f, carry):
        cot_frame(f).wait()
        for q in range(band):
            box_row(f, q, cot_ref[f, 2 * q].astype(F32), cot_ref[f, 2 * q + 1].astype(F32), ((1, q),))
        return carry

    def build_sides(f, carry):
        for j in range(band + 1):
            low = (halo_lo[f] if j == 0 else cot_ref[f, 2 * j - 1]).astype(F32)
            high = (halo_hi[f] if j == band else cot_ref[f, 2 * j]).astype(F32)
            plain = []
            if j < band:
                if j == 1:
                    box_row(f, band + 1, low * lower_w, high, ((2, j),))
                else:
                    plain.append((2, j))
            if j > 0:
                if j == band - 1:
                    box_row(f, band + 2, low, high * upper_w, ((0, j - 1),))
                else:
                    plain.append((0, j - 1))
            box_row(f, j, low, high, plain)
        return carry

    def core_copy(kr):
        return pltpu.make_async_remote_copy(
            src_ref=part.at[kr, 1 - core], dst_ref=core_buf.at[kr], send_sem=core_send.at[kr],
            recv_sem=core_recv.at[kr], device_id={"tile": me + 1 - 2 * core}, device_id_type=MESH,
        )

    def far_copy(kr, d):
        target = lax.rem(chip + d, chips)
        return pltpu.make_async_remote_copy(
            src_ref=send_buf.at[kr, target], dst_ref=recv_buf.at[kr, d - 1],
            send_sem=far_send.at[kr, d - 1], recv_sem=far_recv.at[kr, d - 1],
            device_id={"tile": 2 * target + core}, device_id_type=MESH,
        )

    def kernel_part(kr):
        total = jnp.dot(lhs[...], gh[kr], preferred_element_type=F32)
        total = total + jnp.dot(lhs[...], gl[kr], preferred_element_type=F32)
        for kt in range(3):
            if fused:
                for owner in range(tiles):
                    start = kt * chans + owner * share
                    part[kr, owner % 2, owner // 2, kt] = total[start : start + share]
            else:
                kg_ref[:, (kt * 3 + kr) * 3 * chans : (kt * 3 + kr + 1) * 3 * chans] = total[
                    kt * chans : (kt + 1) * chans
                ]
        if fused:
            core_copy(kr).start()

    def to_owners(kr):
        if fused:
            core_copy(kr).wait_recv()
            send_buf[kr] = (part[kr, core] + core_buf[kr]).astype(BF16)
            for d in range(1, chips):
                far_copy(kr, d).start()

    lax.fori_loop(0, frames, build_middle, 0)
    pl.semaphore_wait(barrier, tiles - 1)

    to_upper = pltpu.make_async_remote_copy(
        src_ref=cot_in.at[:, 2 * band - 1], dst_ref=halo_lo, send_sem=halo_send.at[0],
        recv_sem=halo_recv.at[0], device_id={"tile": lax.rem(me + 1, tiles)}, device_id_type=MESH,
    )
    to_lower = pltpu.make_async_remote_copy(
        src_ref=cot_in.at[:, 0], dst_ref=halo_hi, send_sem=halo_send.at[1],
        recv_sem=halo_recv.at[1], device_id={"tile": lax.rem(me + tiles - 1, tiles)}, device_id_type=MESH,
    )

    @pl.when(me < tiles - 1)
    def _():
        to_upper.start()

    @pl.when(me > 0)
    def _():
        to_lower.start()

    lat_copy.wait()
    for f in range(frames):
        turned = lat_ref[f].reshape(area, chans).T
        for kt in range(3):
            g_frame = f + 2 - kt
            if g_frame < frames:
                lhs[kt * chans : (kt + 1) * chans, g_frame * area : (g_frame + 1) * area] = turned
    for kt in range(2):
        for g_frame in range(2 - kt):
            lhs[kt * chans : (kt + 1) * chans, g_frame * area : (g_frame + 1) * area] = jnp.zeros(
                (chans, area), BF16
            )
    kernel_part(1)
    ramp_copy.wait()
    upper = jnp.full((1, chans), ramp_ref[lax.min(me + 1, tiles - 1)], jnp.int32)
    lower = jnp.full((1, chans), ramp_ref[me], jnp.int32)
    has_upper = jnp.where(me <= tiles - 2, 1.0, 0.0).astype(F32)
    has_lower = jnp.where(me >= 1, 1.0, 0.0).astype(F32)
    upper_w = 1.0 - has_upper * rise(jnp.zeros_like(upper), upper)
    lower_w = 1.0 - has_lower * (1.0 - rise(jnp.full_like(lower, 3), lower))


    @pl.when(me > 0)
    def _():
        to_upper.wait_recv()

    @pl.when(me < tiles - 1)
    def _():
        to_lower.wait_recv()

    lax.fori_loop(0, frames, build_sides, 0)
    to_owners(1)
    kernel_part(0)
    kernel_part(2)
    to_owners(0)

    k_copy.wait()
    for kr in range(3):
        for kc in range(3):
            for kt in range(3):
                kt_ref[kr, kc * chans : (kc + 1) * chans, kt * chans : (kt + 1) * chans] = k_ref[kt, kr, kc].T
    to_owners(2)

    sums = [None] * frames
    for f in range(frames):
        first_kt = max(0, 2 - f)
        rows = slice(f * area, (f + 1) * area)
        spread = jnp.zeros((area, (3 - first_kt) * chans), F32)
        for kr in range(3):
            taps = kt_ref[kr, :, first_kt * chans :]
            spread = spread + jnp.dot(gh[kr, rows], taps, preferred_element_type=F32)
            spread = spread + jnp.dot(gl[kr, rows], taps, preferred_element_type=F32)
        for kt in range(first_kt, 3):
            term = spread[:, (kt - first_kt) * chans : (kt - first_kt + 1) * chans]
            target = f - 2 + kt
            sums[target] = term if sums[target] is None else sums[target] + term
    for f in range(frames):
        lg_ref[f] = sums[f].astype(BF16).reshape(band, width, chans)

    @pl.when(me < tiles - 1)
    def _():
        to_upper.wait_send()

    @pl.when(me > 0)
    def _():
        to_lower.wait_send()

    if fused:
        for kr in (1, 0, 2):
            for d in range(1, chips):
                far_copy(kr, d).wait_recv()
            for kt in range(3):
                total = part[kr, core, chip, kt] + core_buf[kr, chip, kt]
                for d in range(1, chips):
                    total = total + recv_buf[kr, d - 1, kt].astype(F32)
                start = (kt * 3 + kr) * 3 * chans
                kg_ref[:, start : start + 3 * chans] = total / F32(norm)
        for kr in range(3):
            core_copy(kr).wait_send()
            for d in range(1, chips):
                far_copy(kr, d).wait_send()


def shards(tiles, latent, cotangent, kernel, ramp_lengths):
    frames, band, width, chans = latent.shape
    share = chans // tiles
    norm = math.sqrt(4 * frames * band * tiles * width)
    fused = share % 8 == 0 and tiles % 2 == 0
    chips = tiles // 2
    cols = 27 * chans
    dma = pltpu.SemaphoreType.DMA
    scratch = [
        pltpu.SMEM(ramp_lengths.shape, ramp_lengths.dtype),
        pltpu.VMEM(latent.shape, BF16),
        pltpu.VMEM(cotangent.shape, BF16),
        pltpu.VMEM(kernel.shape, BF16),
        dma((3,)),
        dma((frames,)),
        pltpu.VMEM((frames, 2 * width, chans), BF16),
        pltpu.VMEM((frames, 2 * width, chans), BF16),
        pltpu.VMEM((band + 3, 2 * width + 2 * EDGE, chans), F32),
        pltpu.VMEM((3 * chans, frames * band * width), BF16),
        pltpu.VMEM((3, frames * band * width, 3 * chans), BF16),
        pltpu.VMEM((3, frames * band * width, 3 * chans), BF16),
        pltpu.VMEM((3, 3 * chans, 3 * chans), BF16),
        dma((2,)),
        dma((2,)),
    ]
    if fused:
        scratch += [
            pltpu.VMEM((3, 2, chips, 3, share, 3 * chans), F32),
            pltpu.VMEM((3, chips, 3, share, 3 * chans), F32),
            pltpu.VMEM((3, chips, 3, share, 3 * chans), BF16),
            pltpu.VMEM((3, chips - 1, 3, share, 3 * chans), BF16),
            dma((3,)),
            dma((3,)),
            dma((3, chips - 1)),
            dma((3, chips - 1)),
        ]
    vmem = pl.BlockSpec(memory_space=pltpu.VMEM)
    latent_grad, kernel_grad = pl.pallas_call(
        functools.partial(body, tiles, fused, norm),
        out_shape=(
            jax.ShapeDtypeStruct(latent.shape, BF16),
            jax.ShapeDtypeStruct((share if fused else chans, cols), F32),
        ),
        in_specs=[pl.BlockSpec(memory_space=pltpu.HBM)] * 4,
        out_specs=(vmem, vmem),
        scratch_shapes=scratch,
        compiler_params=pltpu.CompilerParams(
            collective_id=0, has_side_effects=True, vmem_limit_bytes=64 * 2**20
        ),
    )(ramp_lengths, latent, cotangent, kernel)
    if not fused:
        kernel_grad = lax.psum_scatter(kernel_grad, "tile", scatter_dimension=0, tiled=True) / F32(norm)
    return latent_grad, kernel_grad


def solution(mesh):
    in_specs = (P("clip", "tile", None, None), P("clip", "tile", None, None), P(), P("clip"))
    out_specs = (P("clip", "tile", None, None), P(("clip", "tile"), None))
    return jax.shard_map(
        functools.partial(shards, mesh.shape["tile"]),
        mesh=mesh, in_specs=in_specs, out_specs=out_specs, check_vma=False,
    )
```

```python
import functools
import math

import jax
import jax.numpy as jnp
from jax import lax
from jax.experimental import pallas as pl
from jax.experimental.pallas import tpu as pltpu
from jax.sharding import PartitionSpec as P

OV = 1
MESH = pl.DeviceIdType.MESH
F32 = jnp.float32
BF16 = jnp.bfloat16
EDGE = 8


def rise(offset, length):
    shift_rows = lax.shift_right_arithmetic(4 * OV - length, jnp.ones_like(length))
    value = (offset - shift_rows + 1).astype(F32) / (length + 1).astype(F32)
    return jnp.clip(value, 0.0, 1.0)


def body(tiles, fused, norm, ramp_in, lat_in, cot_in, k_in, lg_ref, kg_ref, *scratch):
    (ramp_ref, lat_ref, cot_ref, k_ref, in_sem, cot_sem, halo_lo, halo_hi, pad, lhs, gh, gl, kt_ref,
     halo_send, halo_recv) = scratch[:15]
    if fused:
        (part, core_buf, send_buf, recv_buf, core_send, core_recv, far_send, far_recv) = scratch[15:]
    frames, band, width, chans = lat_ref.shape
    wide = 2 * width
    area = band * width
    me = lax.axis_index("tile")
    core = lax.rem(me, 2)
    chip = lax.div(me, 2)
    chips = tiles // 2
    share = chans // tiles

    def cot_frame(f):
        return pltpu.make_async_copy(cot_in.at[f], cot_ref.at[f], cot_sem.at[f])

    ramp_copy = pltpu.make_async_copy(ramp_in, ramp_ref, in_sem.at[0])
    lat_copy = pltpu.make_async_copy(lat_in, lat_ref, in_sem.at[1])
    k_copy = pltpu.make_async_copy(k_in, k_ref, in_sem.at[2])
    ramp_copy.start()
    for f in range(frames):
        cot_frame(f).start()
    lat_copy.start()
    k_copy.start()

    halo_lo[...] = jnp.zeros_like(halo_lo)
    halo_hi[...] = jnp.zeros_like(halo_hi)
    barrier = pltpu.get_barrier_semaphore()
    for d in range(1, tiles):
        pl.semaphore_signal(
            barrier, inc=1, device_id={"tile": lax.rem(me + d, tiles)}, device_id_type=MESH
        )

    pad[:, :EDGE] = jnp.zeros((band + 3, EDGE, chans), F32)
    pad[:, EDGE + wide :] = jnp.zeros((band + 3, EDGE, chans), F32)
    def box_row(f, slot, low, high, targets):
        pad[slot, EDGE : EDGE + wide] = low + high
        left = pad[slot, pl.ds(EDGE - 1, width, stride=2)]
        even = pad[slot, pl.ds(EDGE, width, stride=2)]
        odd = pad[slot, pl.ds(EDGE + 1, width, stride=2)]
        right = pad[slot, pl.ds(EDGE + 2, width, stride=2)]
        for kc, box in enumerate((odd + right, even + odd, left + even)):
            cols = slice(kc * chans, (kc + 1) * chans)
            top = box.astype(BF16)
            rest = (box - top.astype(F32)).astype(BF16)
            for kr, q in targets:
                rows = pl.ds(pl.multiple_of(f * area + q * width, width), width)
                gh[kr, rows, cols] = top
                gl[kr, rows, cols] = rest

    def build_middle(f, carry):
        cot_frame(f).wait()
        for q in range(band):
            box_row(f, q, cot_ref[f, 2 * q].astype(F32), cot_ref[f, 2 * q + 1].astype(F32), ((1, q),))
        return carry

    def build_sides(f, carry):
        for j in range(band + 1):
            low = (halo_lo[f] if j == 0 else cot_ref[f, 2 * j - 1]).astype(F32)
            high = (halo_hi[f] if j == band else cot_ref[f, 2 * j]).astype(F32)
            plain = []
            if j < band:
                if j == 1:
                    box_row(f, band + 1, low * lower_w, high, ((2, j),))
                else:
                    plain.append((2, j))
            if j > 0:
                if j == band - 1:
                    box_row(f, band + 2, low, high * upper_w, ((0, j - 1),))
                else:
                    plain.append((0, j - 1))
            box_row(f, j, low, high, plain)
        return carry

    def core_copy(kr):
        return pltpu.make_async_remote_copy(
            src_ref=part.at[kr, 1 - core], dst_ref=core_buf.at[kr], send_sem=core_send.at[kr],
            recv_sem=core_recv.at[kr], device_id={"tile": me + 1 - 2 * core}, device_id_type=MESH,
        )

    def far_copy(kr, d):
        target = lax.rem(chip + d, chips)
        return pltpu.make_async_remote_copy(
            src_ref=send_buf.at[kr, target], dst_ref=recv_buf.at[kr, d - 1],
            send_sem=far_send.at[kr, d - 1], recv_sem=far_recv.at[kr, d - 1],
            device_id={"tile": 2 * target + core}, device_id_type=MESH,
        )

    def kernel_part(kr):
        total = jnp.dot(lhs[...], gh[kr], preferred_element_type=F32)
        total = total + jnp.dot(lhs[...], gl[kr], preferred_element_type=F32)
        for kt in range(3):
            if fused:
                for owner in range(tiles):
                    start = kt * chans + owner * share
                    part[kr, owner % 2, owner // 2, kt] = total[start : start + share]
            else:
                kg_ref[:, (kt * 3 + kr) * 3 * chans : (kt * 3 + kr + 1) * 3 * chans] = total[
                    kt * chans : (kt + 1) * chans
                ]
        if fused:
            core_copy(kr).start()

    def to_owners(kr):
        if fused:
            core_copy(kr).wait_recv()
            send_buf[kr] = (part[kr, core] + core_buf[kr]).astype(BF16)
            for d in range(1, chips):
                far_copy(kr, d).start()

    pl.semaphore_wait(barrier, tiles - 1)

    to_upper = pltpu.make_async_remote_copy(
        src_ref=cot_in.at[:, 2 * band - 1], dst_ref=halo_lo, send_sem=halo_send.at[0],
        recv_sem=halo_recv.at[0], device_id={"tile": lax.rem(me + 1, tiles)}, device_id_type=MESH,
    )
    to_lower = pltpu.make_async_remote_copy(
        src_ref=cot_in.at[:, 0], dst_ref=halo_hi, send_sem=halo_send.at[1],
        recv_sem=halo_recv.at[1], device_id={"tile": lax.rem(me + tiles - 1, tiles)}, device_id_type=MESH,
    )

    @pl.when(me < tiles - 1)
    def _():
        to_upper.start()

    @pl.when(me > 0)
    def _():
        to_lower.start()

    lax.fori_loop(0, frames, build_middle, 0)
    lat_copy.wait()
    for f in range(frames):
        turned = lat_ref[f].reshape(area, chans).T
        for kt in range(3):
            g_frame = f + 2 - kt
            if g_frame < frames:
                lhs[kt * chans : (kt + 1) * chans, g_frame * area : (g_frame + 1) * area] = turned
    for kt in range(2):
        for g_frame in range(2 - kt):
            lhs[kt * chans : (kt + 1) * chans, g_frame * area : (g_frame + 1) * area] = jnp.zeros(
                (chans, area), BF16
            )
    kernel_part(1)
    ramp_copy.wait()
    upper = jnp.full((1, chans), ramp_ref[lax.min(me + 1, tiles - 1)], jnp.int32)
    lower = jnp.full((1, chans), ramp_ref[me], jnp.int32)
    has_upper = jnp.where(me <= tiles - 2, 1.0, 0.0).astype(F32)
    has_lower = jnp.where(me >= 1, 1.0, 0.0).astype(F32)
    upper_w = 1.0 - has_upper * rise(jnp.zeros_like(upper), upper)
    lower_w = 1.0 - has_lower * (1.0 - rise(jnp.full_like(lower, 3), lower))


    @pl.when(me > 0)
    def _():
        to_upper.wait_recv()

    @pl.when(me < tiles - 1)
    def _():
        to_lower.wait_recv()

    lax.fori_loop(0, frames, build_sides, 0)
    to_owners(1)
    kernel_part(0)
    kernel_part(2)
    to_owners(0)

    k_copy.wait()
    for kr in range(3):
        for kc in range(3):
            for kt in range(3):
                kt_ref[kr, kc * chans : (kc + 1) * chans, kt * chans : (kt + 1) * chans] = k_ref[kt, kr, kc].T
    to_owners(2)

    sums = [None] * frames
    for f in range(frames):
        first_kt = max(0, 2 - f)
        rows = slice(f * area, (f + 1) * area)
        spread = jnp.zeros((area, (3 - first_kt) * chans), F32)
        for kr in range(3):
            taps = kt_ref[kr, :, first_kt * chans :]
            spread = spread + jnp.dot(gh[kr, rows], taps, preferred_element_type=F32)
            spread = spread + jnp.dot(gl[kr, rows], taps, preferred_element_type=F32)
        for kt in range(first_kt, 3):
            term = spread[:, (kt - first_kt) * chans : (kt - first_kt + 1) * chans]
            target = f - 2 + kt
            sums[target] = term if sums[target] is None else sums[target] + term
    for f in range(frames):
        lg_ref[f] = sums[f].astype(BF16).reshape(band, width, chans)

    @pl.when(me < tiles - 1)
    def _():
        to_upper.wait_send()

    @pl.when(me > 0)
    def _():
        to_lower.wait_send()

    if fused:
        for kr in (1, 0, 2):
            for d in range(1, chips):
                far_copy(kr, d).wait_recv()
            for kt in range(3):
                total = part[kr, core, chip, kt] + core_buf[kr, chip, kt]
                for d in range(1, chips):
                    total = total + recv_buf[kr, d - 1, kt].astype(F32)
                start = (kt * 3 + kr) * 3 * chans
                kg_ref[:, start : start + 3 * chans] = total / F32(norm)
        for kr in range(3):
            core_copy(kr).wait_send()
            for d in range(1, chips):
                far_copy(kr, d).wait_send()


def shards(tiles, latent, cotangent, kernel, ramp_lengths):
    frames, band, width, chans = latent.shape
    share = chans // tiles
    norm = math.sqrt(4 * frames * band * tiles * width)
    fused = share % 8 == 0 and tiles % 2 == 0
    chips = tiles // 2
    cols = 27 * chans
    dma = pltpu.SemaphoreType.DMA
    scratch = [
        pltpu.SMEM(ramp_lengths.shape, ramp_lengths.dtype),
        pltpu.VMEM(latent.shape, BF16),
        pltpu.VMEM(cotangent.shape, BF16),
        pltpu.VMEM(kernel.shape, BF16),
        dma((3,)),
        dma((frames,)),
        pltpu.VMEM((frames, 2 * width, chans), BF16),
        pltpu.VMEM((frames, 2 * width, chans), BF16),
        pltpu.VMEM((band + 3, 2 * width + 2 * EDGE, chans), F32),
        pltpu.VMEM((3 * chans, frames * band * width), BF16),
        pltpu.VMEM((3, frames * band * width, 3 * chans), BF16),
        pltpu.VMEM((3, frames * band * width, 3 * chans), BF16),
        pltpu.VMEM((3, 3 * chans, 3 * chans), BF16),
        dma((2,)),
        dma((2,)),
    ]
    if fused:
        scratch += [
            pltpu.VMEM((3, 2, chips, 3, share, 3 * chans), F32),
            pltpu.VMEM((3, chips, 3, share, 3 * chans), F32),
            pltpu.VMEM((3, chips, 3, share, 3 * chans), BF16),
            pltpu.VMEM((3, chips - 1, 3, share, 3 * chans), BF16),
            dma((3,)),
            dma((3,)),
            dma((3, chips - 1)),
            dma((3, chips - 1)),
        ]
    vmem = pl.BlockSpec(memory_space=pltpu.VMEM)
    latent_grad, kernel_grad = pl.pallas_call(
        functools.partial(body, tiles, fused, norm),
        out_shape=(
            jax.ShapeDtypeStruct(latent.shape, BF16),
            jax.ShapeDtypeStruct((share if fused else chans, cols), F32),
        ),
        in_specs=[pl.BlockSpec(memory_space=pltpu.HBM)] * 4,
        out_specs=(vmem, vmem),
        scratch_shapes=scratch,
        compiler_params=pltpu.CompilerParams(
            collective_id=0, has_side_effects=True, vmem_limit_bytes=64 * 2**20
        ),
    )(ramp_lengths, latent, cotangent, kernel)
    if not fused:
        kernel_grad = lax.psum_scatter(kernel_grad, "tile", scatter_dimension=0, tiled=True) / F32(norm)
    return latent_grad, kernel_grad


def solution(mesh):
    in_specs = (P("clip", "tile", None, None), P("clip", "tile", None, None), P(), P("clip"))
    out_specs = (P("clip", "tile", None, None), P(("clip", "tile"), None))
    return jax.shard_map(
        functools.partial(shards, mesh.shape["tile"]),
        mesh=mesh, in_specs=in_specs, out_specs=out_specs, check_vma=False,
    )
```

```python
import functools
import math

import jax
import jax.numpy as jnp
from jax import lax
from jax.experimental import pallas as pl
from jax.experimental.pallas import tpu as pltpu
from jax.sharding import PartitionSpec as P

OV = 1
MESH = pl.DeviceIdType.MESH
F32 = jnp.float32
BF16 = jnp.bfloat16
EDGE = 8


def rise(offset, length):
    shift_rows = lax.shift_right_arithmetic(4 * OV - length, jnp.ones_like(length))
    value = (offset - shift_rows + 1).astype(F32) / (length + 1).astype(F32)
    return jnp.clip(value, 0.0, 1.0)


def body(tiles, fused, norm, ramp_in, lat_in, cot_in, k_in, lg_ref, kg_ref, *scratch):
    (ramp_ref, lat_ref, cot_ref, k_ref, in_sem, cot_sem, halo_lo, halo_hi, pad, lhs, gh, gl, kt_ref,
     halo_send, halo_recv) = scratch[:15]
    if fused:
        (part, core_buf, send_buf, recv_buf, core_send, core_recv, far_send, far_recv) = scratch[15:]
    frames, band, width, chans = lat_ref.shape
    wide = 2 * width
    area = band * width
    me = lax.axis_index("tile")
    core = lax.rem(me, 2)
    chip = lax.div(me, 2)
    chips = tiles // 2
    share = chans // tiles

    def cot_frame(f):
        return pltpu.make_async_copy(cot_in.at[f], cot_ref.at[f], cot_sem.at[f])

    ramp_copy = pltpu.make_async_copy(ramp_in, ramp_ref, in_sem.at[0])
    lat_copy = pltpu.make_async_copy(lat_in, lat_ref, in_sem.at[1])
    k_copy = pltpu.make_async_copy(k_in, k_ref, in_sem.at[2])
    ramp_copy.start()
    for f in range(frames):
        cot_frame(f).start()
    lat_copy.start()
    k_copy.start()

    halo_lo[...] = jnp.zeros_like(halo_lo)
    halo_hi[...] = jnp.zeros_like(halo_hi)
    barrier = pltpu.get_barrier_semaphore()
    for d in range(1, tiles):
        pl.semaphore_signal(
            barrier, inc=1, device_id={"tile": lax.rem(me + d, tiles)}, device_id_type=MESH
        )

    pad[:, :EDGE] = jnp.zeros((band + 3, EDGE, chans), F32)
    pad[:, EDGE + wide :] = jnp.zeros((band + 3, EDGE, chans), F32)
    def box_row(f, slot, low, high, targets):
        pad[slot, EDGE : EDGE + wide] = low + high
        left = pad[slot, pl.ds(EDGE - 1, width, stride=2)]
        even = pad[slot, pl.ds(EDGE, width, stride=2)]
        odd = pad[slot, pl.ds(EDGE + 1, width, stride=2)]
        right = pad[slot, pl.ds(EDGE + 2, width, stride=2)]
        for kc, box in enumerate((odd + right, even + odd, left + even)):
            cols = slice(kc * chans, (kc + 1) * chans)
            top = box.astype(BF16)
            rest = (box - top.astype(F32)).astype(BF16)
            for kr, q in targets:
                rows = pl.ds(pl.multiple_of(f * area + q * width, width), width)
                gh[kr, rows, cols] = top
                gl[kr, rows, cols] = rest

    def build_middle(f, carry):
        cot_frame(f).wait()
        for q in range(band):
            box_row(f, q, cot_ref[f, 2 * q].astype(F32), cot_ref[f, 2 * q + 1].astype(F32), ((1, q),))
        return carry

    def build_sides(f, carry):
        for j in range(band + 1):
            low = (halo_lo[f] if j == 0 else cot_ref[f, 2 * j - 1]).astype(F32)
            high = (halo_hi[f] if j == band else cot_ref[f, 2 * j]).astype(F32)
            plain = []
            if j < band:
                if j == 1:
                    box_row(f, band + 1, low * lower_w, high, ((2, j),))
                else:
                    plain.append((2, j))
            if j > 0:
                if j == band - 1:
                    box_row(f, band + 2, low, high * upper_w, ((0, j - 1),))
                else:
                    plain.append((0, j - 1))
            box_row(f, j, low, high, plain)
        return carry

    def core_copy(kr):
        return pltpu.make_async_remote_copy(
            src_ref=part.at[kr, 1 - core], dst_ref=core_buf.at[kr], send_sem=core_send.at[kr],
            recv_sem=core_recv.at[kr], device_id={"tile": me + 1 - 2 * core}, device_id_type=MESH,
        )

    def far_copy(kr, d):
        target = lax.rem(chip + d, chips)
        return pltpu.make_async_remote_copy(
            src_ref=send_buf.at[kr, target], dst_ref=recv_buf.at[kr, d - 1],
            send_sem=far_send.at[kr, d - 1], recv_sem=far_recv.at[kr, d - 1],
            device_id={"tile": 2 * target + core}, device_id_type=MESH,
        )

    def kernel_part(kr):
        total = jnp.dot(lhs[...], gh[kr], preferred_element_type=F32)
        total = total + jnp.dot(lhs[...], gl[kr], preferred_element_type=F32)
        for kt in range(3):
            if fused:
                for owner in range(tiles):
                    start = kt * chans + owner * share
                    part[kr, owner % 2, owner // 2, kt] = total[start : start + share]
            else:
                kg_ref[:, (kt * 3 + kr) * 3 * chans : (kt * 3 + kr + 1) * 3 * chans] = total[
                    kt * chans : (kt + 1) * chans
                ]
        if fused:
            core_copy(kr).start()

    def to_owners(kr):
        if fused:
            core_copy(kr).wait_recv()
            send_buf[kr] = (part[kr, core] + core_buf[kr]).astype(BF16)
            for d in range(1, chips):
                far_copy(kr, d).start()

    pl.semaphore_wait(barrier, tiles - 1)

    to_upper = pltpu.make_async_remote_copy(
        src_ref=cot_in.at[:, 2 * band - 1], dst_ref=halo_lo, send_sem=halo_send.at[0],
        recv_sem=halo_recv.at[0], device_id={"tile": lax.rem(me + 1, tiles)}, device_id_type=MESH,
    )
    to_lower = pltpu.make_async_remote_copy(
        src_ref=cot_in.at[:, 0], dst_ref=halo_hi, send_sem=halo_send.at[1],
        recv_sem=halo_recv.at[1], device_id={"tile": lax.rem(me + tiles - 1, tiles)}, device_id_type=MESH,
    )

    @pl.when(me < tiles - 1)
    def _():
        to_upper.start()

    @pl.when(me > 0)
    def _():
        to_lower.start()

    lax.fori_loop(0, frames, build_middle, 0)
    lat_copy.wait()
    for f in range(frames):
        turned = lat_ref[f].reshape(area, chans).T
        for kt in range(3):
            g_frame = f + 2 - kt
            if g_frame < frames:
                lhs[kt * chans : (kt + 1) * chans, g_frame * area : (g_frame + 1) * area] = turned
    for kt in range(2):
        for g_frame in range(2 - kt):
            lhs[kt * chans : (kt + 1) * chans, g_frame * area : (g_frame + 1) * area] = jnp.zeros(
                (chans, area), BF16
            )
    kernel_part(1)
    k_copy.wait()
    for kr in range(3):
        for kc in range(3):
            for kt in range(3):
                kt_ref[kr, kc * chans : (kc + 1) * chans, kt * chans : (kt + 1) * chans] = k_ref[kt, kr, kc].T
    to_owners(1)
    ramp_copy.wait()
    upper = jnp.full((1, chans), ramp_ref[lax.min(me + 1, tiles - 1)], jnp.int32)
    lower = jnp.full((1, chans), ramp_ref[me], jnp.int32)
    has_upper = jnp.where(me <= tiles - 2, 1.0, 0.0).astype(F32)
    has_lower = jnp.where(me >= 1, 1.0, 0.0).astype(F32)
    upper_w = 1.0 - has_upper * rise(jnp.zeros_like(upper), upper)
    lower_w = 1.0 - has_lower * (1.0 - rise(jnp.full_like(lower, 3), lower))


    @pl.when(me > 0)
    def _():
        to_upper.wait_recv()

    @pl.when(me < tiles - 1)
    def _():
        to_lower.wait_recv()

    lax.fori_loop(0, frames, build_sides, 0)
    kernel_part(0)
    kernel_part(2)
    to_owners(0)


    sums = [None] * frames
    for f in range(frames):
        first_kt = max(0, 2 - f)
        rows = slice(f * area, (f + 1) * area)
        spread = jnp.zeros((area, (3 - first_kt) * chans), F32)
        for kr in range(3):
            taps = kt_ref[kr, :, first_kt * chans :]
            spread = spread + jnp.dot(gh[kr, rows], taps, preferred_element_type=F32)
            spread = spread + jnp.dot(gl[kr, rows], taps, preferred_element_type=F32)
        for kt in range(first_kt, 3):
            term = spread[:, (kt - first_kt) * chans : (kt - first_kt + 1) * chans]
            target = f - 2 + kt
            sums[target] = term if sums[target] is None else sums[target] + term
        if f == 0:
            to_owners(2)
    for f in range(frames):
        lg_ref[f] = sums[f].astype(BF16).reshape(band, width, chans)

    @pl.when(me < tiles - 1)
    def _():
        to_upper.wait_send()

    @pl.when(me > 0)
    def _():
        to_lower.wait_send()

    if fused:
        for kr in (1, 0, 2):
            for d in range(1, chips):
                far_copy(kr, d).wait_recv()
            for kt in range(3):
                total = part[kr, core, chip, kt] + core_buf[kr, chip, kt]
                for d in range(1, chips):
                    total = total + recv_buf[kr, d - 1, kt].astype(F32)
                start = (kt * 3 + kr) * 3 * chans
                kg_ref[:, start : start + 3 * chans] = total / F32(norm)
        for kr in range(3):
            core_copy(kr).wait_send()
            for d in range(1, chips):
                far_copy(kr, d).wait_send()


def shards(tiles, latent, cotangent, kernel, ramp_lengths):
    frames, band, width, chans = latent.shape
    share = chans // tiles
    norm = math.sqrt(4 * frames * band * tiles * width)
    fused = share % 8 == 0 and tiles % 2 == 0
    chips = tiles // 2
    cols = 27 * chans
    dma = pltpu.SemaphoreType.DMA
    scratch = [
        pltpu.SMEM(ramp_lengths.shape, ramp_lengths.dtype),
        pltpu.VMEM(latent.shape, BF16),
        pltpu.VMEM(cotangent.shape, BF16),
        pltpu.VMEM(kernel.shape, BF16),
        dma((3,)),
        dma((frames,)),
        pltpu.VMEM((frames, 2 * width, chans), BF16),
        pltpu.VMEM((frames, 2 * width, chans), BF16),
        pltpu.VMEM((band + 3, 2 * width + 2 * EDGE, chans), F32),
        pltpu.VMEM((3 * chans, frames * band * width), BF16),
        pltpu.VMEM((3, frames * band * width, 3 * chans), BF16),
        pltpu.VMEM((3, frames * band * width, 3 * chans), BF16),
        pltpu.VMEM((3, 3 * chans, 3 * chans), BF16),
        dma((2,)),
        dma((2,)),
    ]
    if fused:
        scratch += [
            pltpu.VMEM((3, 2, chips, 3, share, 3 * chans), F32),
            pltpu.VMEM((3, chips, 3, share, 3 * chans), F32),
            pltpu.VMEM((3, chips, 3, share, 3 * chans), BF16),
            pltpu.VMEM((3, chips - 1, 3, share, 3 * chans), BF16),
            dma((3,)),
            dma((3,)),
            dma((3, chips - 1)),
            dma((3, chips - 1)),
        ]
    vmem = pl.BlockSpec(memory_space=pltpu.VMEM)
    latent_grad, kernel_grad = pl.pallas_call(
        functools.partial(body, tiles, fused, norm),
        out_shape=(
            jax.ShapeDtypeStruct(latent.shape, BF16),
            jax.ShapeDtypeStruct((share if fused else chans, cols), F32),
        ),
        in_specs=[pl.BlockSpec(memory_space=pltpu.HBM)] * 4,
        out_specs=(vmem, vmem),
        scratch_shapes=scratch,
        compiler_params=pltpu.CompilerParams(
            collective_id=0, has_side_effects=True, vmem_limit_bytes=64 * 2**20
        ),
    )(ramp_lengths, latent, cotangent, kernel)
    if not fused:
        kernel_grad = lax.psum_scatter(kernel_grad, "tile", scatter_dimension=0, tiled=True) / F32(norm)
    return latent_grad, kernel_grad


def solution(mesh):
    in_specs = (P("clip", "tile", None, None), P("clip", "tile", None, None), P(), P("clip"))
    out_specs = (P("clip", "tile", None, None), P(("clip", "tile"), None))
    return jax.shard_map(
        functools.partial(shards, mesh.shape["tile"]),
        mesh=mesh, in_specs=in_specs, out_specs=out_specs, check_vma=False,
    )
```
